32 devices in a mesh: section: 4 (over y, x), row: 8 (over z, core).
Axes of the slice: x: 2, y: 2, z: 4, core: 2. Of those that a mesh axis runs over, the one named last changes fastest.
Arguments:
- in_flight: bfloat16 [2, 4, 16, 128, 256], P(None, 'section', 'row'), may hold values from -6 to 6
- fresh: bfloat16 [2, 3, 16, 128, 256], P(None, None, 'row'), may hold values from -6 to 6
- saved_inputs: bfloat16 [2, 4, 4, 16, 128, 256], P(None, None, 'section', 'row'), may hold values from -6 to 6
- saved_hidden: bfloat16 [2, 4, 4, 16, 128, 256], P(None, None, 'section', 'row'), may hold values from 0 to 2
- masks: int32 [2, 4, 4, 2, 16, 16, 256], P(None, None, 'section', None, 'row'), may hold values from 0 to 255
- weights: bfloat16 [4, 2, 2304, 256], P('section'), may hold values from -0.125 to 0.125
Outputs:
- grads: bfloat16 [2, 4, 4, 16, 128, 256], P(None, None, 'section', 'row')
- weight_grads: float32 [4, 2, 2304, 256], P('section', None, 'row')
The draws below stay inside these ranges and needn't reach their ends.
Inputs may be any that keep to these rules, and one draw needn't show every extreme that they name: `masks`: bit q of entry [r, t, p, k, i, j, c] is the gate at image row i, column 8 j + q, channel c; k = 0 gates the first convolution's output, k = 1 the residual sum.
All inputs are finite; a program needn't handle non-finite values.
Results may differ from the reference program's by a relative error of at most 0.014.
Values may be sent and summed in bfloat16 or wider, within the bound.
A program may use at most 192 MiB of HBM per device.

```python
import math
import jax
import jax.numpy as jnp
from jax import lax

C = 256
COLS = 128
TICKS = 4
SECTIONS = 4
ROWS = 16


def touch_ends(drawn, key, low, largest):
    longest = drawn.shape.index(max(drawn.shape))
    spots = []
    for shift in (0, 1):
        where = [jax.random.randint(jax.random.fold_in(key, axis), (), 0, length) for axis, length in enumerate(drawn.shape)]
        where[longest] = (where[longest] + shift) % drawn.shape[longest]
        spots.append(tuple(where))
    return drawn.at[spots[0]].set(low).at[spots[1]].set(largest)


def block_scale(stream_key, shape, cuts, smallest, high):
    level, own = 1.0, jax.random.fold_in(stream_key, 6)
    for axis_at, blocks in cuts:
        steps = jnp.exp(jax.random.uniform(jax.random.fold_in(own, axis_at), (blocks,), jnp.float32, smallest / len(cuts), high / len(cuts)))
        level = level * jnp.repeat(steps, shape[axis_at] // blocks).reshape([-1 if axis == axis_at else 1 for axis in range(len(shape))])
    return level


def gaussian(stream_key, shape, scale, most, cuts=(), held_as=jnp.bfloat16):
    loudness = block_scale(stream_key, shape, cuts, -0.22, 0.18) if cuts else 1.0
    values = jax.random.normal(stream_key, shape, jnp.float32) * scale * loudness
    return jnp.minimum(jnp.maximum(values, -most), most).astype(held_as)


def setup_inputs(seed: int = 0) -> dict:
    keys = jax.random.split(jax.random.key(seed), 7)
    return {
        "in_flight": gaussian(keys[0], (2, SECTIONS, ROWS, COLS, C), 1.0, 6.0, ((1, 4), (2, 8))),
        "fresh": gaussian(keys[1], (2, TICKS - 1, ROWS, COLS, C), 1.0, 6.0, ((2, 8),)),
        "saved_inputs": gaussian(keys[2], (2, TICKS, SECTIONS, ROWS, COLS, C), 1.0, 6.0, ((2, 4), (3, 8))),
        "saved_hidden": jnp.clip(2.0 * jax.random.uniform(keys[3], (2, TICKS, SECTIONS, ROWS, COLS, C), jnp.float32) ** block_scale(keys[3], (2, TICKS, SECTIONS, ROWS, COLS, C), ((2, 4), (3, 8)), -0.2, 0.2), 0.0, 2.0).astype(jnp.bfloat16),
        "masks": touch_ends(jax.random.randint(keys[4], (2, TICKS, SECTIONS, 2, ROWS, COLS // 8, C), 0, 256), jax.random.fold_in(keys[4], 1), 0, 255).astype(jnp.int32),
        "weights": gaussian(keys[5], (SECTIONS, 2, 9 * C, C), (9 * C) ** -0.5, 0.125, ((0, 4),)),
    }


def unpack(words):
    bit_index = jnp.arange(8, dtype=jnp.int32)
    spread = jnp.bitwise_and(jnp.right_shift(words[..., None, :], bit_index[:, None]), 1)
    return spread.reshape(words.shape[:-2] + (words.shape[-2] * 8, words.shape[-1])).astype(jnp.bfloat16)

def window_patches(padded):
    row_count = padded.shape[-3] - 2
    col_count = padded.shape[-2] - 2
    pieces = [padded[..., shift_row:shift_row + row_count, shift_col:shift_col + col_count, :] for shift_row in range(3) for shift_col in range(3)]
    return jnp.concatenate(pieces, axis=-1)

def transpose_conv(cotangent, flipped):
    row_count, col_count, channels = cotangent.shape
    windows = window_patches(jnp.pad(cotangent, ((1, 1), (1, 1), (0, 0))))
    windows = windows.reshape(row_count * col_count, 9, channels).astype(jnp.float32)
    result = jnp.einsum('pkc,kdc->pd', windows, flipped.astype(jnp.float32))
    return result.reshape(row_count, col_count, channels)

def weight_grad(saved, cotangent):
    row_count, col_count, channels = cotangent.shape
    windows = window_patches(jnp.pad(saved, ((1, 1), (1, 1), (0, 0))))
    windows = windows.reshape(row_count * col_count, 9 * channels)
    return jnp.dot(windows.T, cotangent.reshape(row_count * col_count, channels), preferred_element_type=jnp.float32)

def block_backward(operands):
    cotangent, saved_input, saved_mid, words, flipped = operands
    gates = unpack(words)
    gated_out = cotangent * gates[1]
    mid_grad = transpose_conv(gated_out, flipped[1])
    gated_mid = (mid_grad * gates[0]).astype(jnp.bfloat16)
    back_grad = transpose_conv(gated_mid, flipped[0])
    input_grad = (gated_out.astype(jnp.float32) + back_grad).astype(jnp.bfloat16)
    kernel_terms = jnp.stack([weight_grad(saved_input, gated_mid), weight_grad(saved_mid, gated_out)])
    return (input_grad, kernel_terms)

def reference(in_flight, fresh, saved_inputs, saved_hidden, masks, weights):
    channels = weights.shape[-1]
    sections = weights.shape[0]
    flipped = weights.reshape(sections, 2, 3, 3, channels, channels)[:, :, ::-1, ::-1]
    flipped = flipped.reshape(sections, 2, 9, channels, channels)
    chosen = (flipped, flipped[::-1])
    states = (in_flight[0], in_flight[1])
    totals = [jnp.zeros((sections, 2, 9 * channels, channels), jnp.float32) for replica in range(2)]
    outputs = []
    produced = []
    for tick_index in range(TICKS):
        if tick_index > 0:
            lower = jnp.concatenate([produced[0][1:], fresh[0, tick_index - 1][None]], axis=0)
            upper = jnp.concatenate([fresh[1, tick_index - 1][None], produced[1][:-1]], axis=0)
            states = (lower, upper)
        produced = []
        for replica in range(2):
            input_grad, kernel_terms = lax.map(block_backward, (states[replica], saved_inputs[replica, tick_index], saved_hidden[replica, tick_index], masks[replica, tick_index], chosen[replica]))
            produced.append(input_grad)
            totals[replica] = totals[replica] + kernel_terms
        outputs.append(jnp.stack(produced))
    grads = jnp.stack(outputs, axis=1)
    scale = 1.0 / math.sqrt(2 * TICKS * ROWS * COLS)
    weight_grads = (totals[0] + totals[1][::-1]) * scale
    return (grads, weight_grads)
```

```python
import functools
import math

import jax
import jax.numpy as jnp
from jax import lax
from jax.experimental import pallas as pl
from jax.experimental.pallas import tpu as pltpu
from jax.sharding import PartitionSpec as P

F32 = jnp.float32
BF16 = jnp.bfloat16
VMEM = pl.BlockSpec(memory_space=pltpu.VMEM)
SMEM = pl.BlockSpec(memory_space=pltpu.SMEM)


def gate_of(words):
    groups, channels = words.shape
    bit = lax.broadcasted_iota(jnp.int32, (8, channels), 0)
    pieces = [
        jnp.bitwise_and(
            jnp.right_shift(jnp.broadcast_to(words[j : j + 1, :], (8, channels)), bit), 1
        )
        for j in range(groups)
    ]
    return jnp.concatenate(pieces, axis=0).astype(F32)


def shifted(x, step):
    cols = x.shape[0]
    rolled = pltpu.roll(x, (-step) % cols, 0)
    at = lax.broadcasted_iota(jnp.int32, x.shape, 0)
    edge = cols - 1 if step == 1 else 0
    return jnp.where(at == edge, 0.0, rolled)


def gate_kernel(last_ref, handed_ref, fresh_ref, words_ref, out_ref):
    replicas, rows = out_ref.shape[:2]
    is_last = last_ref[0] == 1
    for r in range(replicas):
        for i in range(rows):
            state = jnp.where(is_last, fresh_ref[r, i].astype(F32), handed_ref[r, i].astype(F32))
            out_ref[r, i] = (state * gate_of(words_ref[r, i])).astype(BF16)


def transposed(core_ref, above_ref, below_ref, w_ref):
    replicas, rows, cols, channels = core_ref.shape
    padded = [
        [above_ref[r]] + [core_ref[r, i] for i in range(rows)] + [below_ref[r]]
        for r in range(replicas)
    ]
    lhs = jnp.concatenate(
        [
            jnp.concatenate(
                [padded[r][i - u + 2] for r in range(replicas) for i in range(rows)], axis=0
            )
            for u in range(3)
        ],
        axis=1,
    )
    parts = []
    for v in range(3):
        rhs = jnp.concatenate(
            [w_ref[pl.ds((u * 3 + v) * channels, channels), :] for u in range(3)], axis=1
        )
        parts.append(
            lax.dot_general(lhs, rhs, (((1,), (1,)), ((), ())), preferred_element_type=F32)
        )
    out = []
    for n in range(replicas * rows):
        low, mid, high = (part[n * cols : (n + 1) * cols] for part in parts)
        out.append(shifted(low, 1) + mid + shifted(high, -1))
    return out


def mid_kernel(core_ref, above_ref, below_ref, w_ref, words_ref, out_ref):
    replicas, rows = core_ref.shape[:2]
    back = transposed(core_ref, above_ref, below_ref, w_ref)
    for r in range(replicas):
        for i in range(rows):
            out_ref[r, i] = (back[r * rows + i] * gate_of(words_ref[r, i])).astype(BF16)


def out_kernel(core_ref, above_ref, below_ref, w_ref, skip_ref, out_ref):
    replicas, rows = core_ref.shape[:2]
    back = transposed(core_ref, above_ref, below_ref, w_ref)
    for r in range(replicas):
        for i in range(rows):
            out_ref[r, i] = (skip_ref[r, i].astype(F32) + back[r * rows + i]).astype(BF16)


def grad_kernel(ticks, *refs):
    own_ref, other_ref = refs[:2]
    cores = refs[2 : 2 + ticks]
    aboves = refs[2 + ticks : 2 + 2 * ticks]
    belows = refs[2 + 2 * ticks : 2 + 3 * ticks]
    out_ref = refs[2 + 3 * ticks]
    xt_ref = refs[3 + 3 * ticks]
    y_ref = refs[4 + 3 * ticks]
    replicas, rows, cols, channels = cores[0].shape
    span = replicas * rows * cols
    for t in range(ticks):
        for r in range(replicas):
            for i in range(rows):
                x = (own_ref if r == 0 else other_ref)[t, i]
                at = t * span + (r * rows + i) * cols
                xt_ref[:, at : at + cols] = x.T
    for v in range(3):
        for t in range(ticks):
            for r in range(replicas):
                padded = [aboves[t][r]] + [cores[t][r, i] for i in range(rows)] + [belows[t][r]]
                for n in range(rows + 2):
                    line = padded[n]
                    if v != 1:
                        line = shifted(line.astype(F32), 1 - v).astype(BF16)
                    for u in range(3):
                        i = n + u - 2
                        if 0 <= i < rows:
                            at = t * span + (r * rows + i) * cols
                            y_ref[at : at + cols, u * channels : (u + 1) * channels] = line
        term = jnp.dot(xt_ref[...], y_ref[...], preferred_element_type=F32)
        for u in range(3):
            out_ref[(u * 3 + v) * channels : (u * 3 + v + 1) * channels, :] = term[
                :, u * channels : (u + 1) * channels
            ].astype(BF16)


def params(limit):
    return pltpu.CompilerParams(vmem_limit_bytes=limit << 20)


def call(kernel, out_shape, flops, *operands, specs=None, scratch=(), limit=24):
    moved = sum(math.prod(o.shape) * o.dtype.itemsize for o in operands)
    return pl.pallas_call(
        kernel,
        out_shape=out_shape,
        in_specs=specs or [VMEM] * len(operands),
        out_specs=VMEM,
        scratch_shapes=scratch,
        compiler_params=params(limit),
        cost_estimate=pl.CostEstimate(flops=flops, bytes_accessed=moved, transcendentals=0),
    )(*operands)


def edges(x):
    size = lax.axis_size("row")
    down = [(i, i + 1) for i in range(size - 1)]
    up = [(j, i) for i, j in down]
    return lax.ppermute(x[:, -1], "row", down), lax.ppermute(x[:, 0], "row", up)


def mirrored(x):
    size = lax.axis_size("section")
    return lax.ppermute(x, "section", [(i, size - 1 - i) for i in range(size)])


def per_device(in_flight, fresh, saved_inputs, saved_hidden, masks, weights):
    sections = lax.axis_size("section")
    bands = lax.axis_size("row")
    position = lax.axis_index("section")
    replicas, ticks = saved_inputs.shape[:2]
    rows, cols, channels = saved_inputs.shape[3:]
    w1, w2 = weights[0, 0], weights[0, 1]
    own_masks = masks[0, :, 0]
    other_flight = mirrored(in_flight[1, 0])
    other_masks = [mirrored(masks[1, t, 0]) for t in range(ticks)]
    other_hidden = mirrored(saved_hidden[1, :, 0])
    other_inputs = mirrored(saved_inputs[1, :, 0])
    is_last = (position == sections - 1).astype(jnp.int32).reshape(1)
    below = [(i, i - 1) for i in range(1, sections)]
    shape = jax.ShapeDtypeStruct((replicas, rows, cols, channels), BF16)
    conv_flops = 2 * replicas * rows * cols * 9 * channels * channels
    handed = jnp.stack([in_flight[0, 0], other_flight])
    lines = []
    outs = [[], []]
    for t in range(ticks):
        words = jnp.stack([own_masks[t], other_masks[t]])
        entering = handed if t == 0 else fresh[:, t - 1]
        g2 = call(
            gate_kernel, shape, 1, is_last, handed, entering, words[:, 1],
            specs=[SMEM, VMEM, VMEM, VMEM],
        )
        a2, b2 = edges(g2)
        g1 = call(mid_kernel, shape, conv_flops, g2, a2, b2, w2, words[:, 0])
        a1, b1 = edges(g1)
        produced = call(out_kernel, shape, conv_flops, g1, a1, b1, w1, g2)
        if t < ticks - 1:
            handed = lax.ppermute(produced, "section", below)
        outs[0].append(produced[0])
        outs[1].append(mirrored(produced[1]))
        lines.append((g2, a2, b2, g1, a1, b1))
    scale = 1.0 / math.sqrt(replicas * ticks * rows * bands * cols)
    span = replicas * rows * cols * ticks
    scratch = [pltpu.VMEM((channels, span), BF16), pltpu.VMEM((span, 3 * channels), BF16)]
    term_shape = jax.ShapeDtypeStruct((9 * channels, channels), BF16)

    def term(own, other, first):
        return call(
            functools.partial(grad_kernel, ticks), term_shape, conv_flops * ticks,
            own, other,
            *[l[first] for l in lines], *[l[first + 1] for l in lines], *[l[first + 2] for l in lines],
            scratch=scratch, limit=40,
        )

    def scattered(x):
        return lax.psum_scatter(x, "row", scatter_dimension=0, tiled=True).astype(F32) * scale

    second = scattered(term(saved_hidden[0, :, 0], other_hidden, 0))
    first = scattered(term(saved_inputs[0, :, 0], other_inputs, 3))
    grads = jnp.stack([jnp.stack(o) for o in outs])[:, :, None]
    return grads, jnp.stack([first, second])[None]


def solution(mesh):
    return jax.shard_map(
        per_device,
        mesh=mesh,
        in_specs=(
            P(None, "section", "row", None, None),
            P(None, None, "row", None, None),
            P(None, None, "section", "row", None, None),
            P(None, None, "section", "row", None, None),
            P(None, None, "section", None, "row", None, None),
            P("section", None, None, None),
        ),
        out_specs=(P(None, None, "section", "row", None, None), P("section", None, "row", None)),
        check_vma=False,
    )
```

```python
import math

import jax
import jax.numpy as jnp
from jax import lax
from jax.experimental import pallas as pl
from jax.experimental.pallas import tpu as pltpu
from jax.sharding import PartitionSpec as P

F32 = jnp.float32
BF16 = jnp.bfloat16
VMEM = pl.BlockSpec(memory_space=pltpu.VMEM)


def gate_of(words):
    groups, channels = words.shape
    bit = lax.broadcasted_iota(jnp.int32, (8, channels), 0)
    pieces = [
        jnp.bitwise_and(
            jnp.right_shift(jnp.broadcast_to(words[j : j + 1, :], (8, channels)), bit), 1
        )
        for j in range(groups)
    ]
    return jnp.concatenate(pieces, axis=0).astype(F32)


def shifted(x, step):
    cols = x.shape[0]
    rolled = pltpu.roll(x, (-step) % cols, 0)
    at = lax.broadcasted_iota(jnp.int32, x.shape, 0)
    edge = cols - 1 if step == 1 else 0
    return jnp.where(at == edge, 0.0, rolled)


def transposed(core_ref, above_ref, below_ref, w_ref, w_at):
    replicas, rows, cols, channels = core_ref.shape
    padded = [
        [above_ref[r]] + [core_ref[r, i] for i in range(rows)] + [below_ref[r]]
        for r in range(replicas)
    ]
    lhs = jnp.concatenate(
        [
            jnp.concatenate(
                [padded[r][i - u + 2] for r in range(replicas) for i in range(rows)], axis=0
            )
            for u in range(3)
        ],
        axis=1,
    )
    parts = []
    for v in range(3):
        rhs = jnp.concatenate(
            [w_ref[0, w_at, pl.ds((u * 3 + v) * channels, channels), :] for u in range(3)], axis=1
        )
        parts.append(
            lax.dot_general(lhs, rhs, (((1,), (1,)), ((), ())), preferred_element_type=F32)
        )
    out = []
    for n in range(replicas * rows):
        low, mid, high = (part[n * cols : (n + 1) * cols] for part in parts)
        out.append(shifted(low, 1) + mid + shifted(high, -1))
    return out


MESH = pl.DeviceIdType.MESH


def relay_kernel(
    flight_ref, fresh_ref, inputs_ref, hidden_ref, masks_ref, w_ref,
    grads_ref, wgrads_ref,
    flight_in, words_in, inputs_in, hidden_in, handed, produced,
    g_ref, above, below, total, term, pair_in, pair_sum, chip_in, xt, yt,
    flight_sem, words_sem, saved_sem, hand_sem, back_sem, up_sem, down_sem, pair_sem, chip_sem,
):
    sections, bands = lax.axis_size("section"), lax.axis_size("row")
    sec, row = lax.axis_index("section"), lax.axis_index("row")
    ticks, _, rows, cols, channels = inputs_ref.shape[1:]
    chips = bands // 2
    chip, core = row // 2, row % 2
    mirror = sections - 1 - sec
    share = 9 * channels // bands
    scale = 1.0 / math.sqrt(2 * ticks * rows * bands * cols)

    above[...] = jnp.zeros_like(above)
    below[...] = jnp.zeros_like(below)
    barrier = pltpu.get_barrier_semaphore()
    peers = [(sec, (row + d) % bands) for d in range(1, bands)]
    peers += [(mirror, row), ((sec + 1) % sections, row), ((sec + sections - 1) % sections, row)]
    for peer in peers:
        pl.semaphore_signal(barrier, inc=1, device_id=peer, device_id_type=MESH)
    pl.semaphore_wait(barrier, len(peers))

    waits = []

    def copy(source, target, sems, device):
        return pltpu.make_async_remote_copy(
            src_ref=source, dst_ref=target, send_sem=sems.at[0], recv_sem=sems.at[1],
            device_id=device, device_id_type=MESH,
        )

    def send(c, when=None):
        if when is None:
            c.start()
        else:
            pl.when(when)(c.start)
        waits.append((c, when))
        return c

    def arrive(c, when=None):
        if when is None:
            c.wait_recv()
        else:
            pl.when(when)(c.wait_recv)

    other = (mirror, row)
    flight_copy = send(copy(flight_ref.at[1, 0], flight_in, flight_sem, other))
    words_copies = [
        copy(masks_ref.at[1, t, 0], words_in.at[t], words_sem.at[t], other) for t in range(ticks)
    ]
    hidden_copies = [
        copy(hidden_ref.at[1, t, 0], hidden_in.at[t], saved_sem.at[1, t], other)
        for t in range(ticks)
    ]
    inputs_copies = [
        copy(inputs_ref.at[1, t, 0], inputs_in.at[t], saved_sem.at[0, t], other)
        for t in range(ticks)
    ]
    send(words_copies[0])
    queue = [
        words_copies[1:2] + hidden_copies[:2],
        words_copies[2:3] + hidden_copies[2:] + inputs_copies[:1],
        words_copies[3:] + inputs_copies[1:3],
        inputs_copies[3:],
    ]

    has_above, has_below = row > 0, row < bands - 1
    up_peer = (sec, jnp.maximum(row - 1, 0))
    down_peer = (sec, jnp.minimum(row + 1, bands - 1))

    def words(r, t, k, i):
        return masks_ref[0, t, 0, k, i] if r == 0 else words_in[t, k, i]

    def exchange(k, t):
        pairs = []
        for r in range(2):
            up = copy(g_ref.at[k, t, r, 0], below.at[k, t, r], up_sem.at[k, t, r], up_peer)
            down = copy(
                g_ref.at[k, t, r, rows - 1], above.at[k, t, r], down_sem.at[k, t, r], down_peer
            )
            send(up, has_above)
            send(down, has_below)
            pairs.append((up, down))
        return pairs

    def arrived(pairs):
        for up, down in pairs:
            arrive(up, has_below)
            arrive(down, has_above)

    def gate(t, state):
        for r in range(2):
            for i in range(rows):
                value = state(r, i).astype(F32) * gate_of(words(r, t, 1, i))
                g_ref[1, t, r, i] = value.astype(BF16)

    def add_terms(k, t):
        own, far = (inputs_ref, inputs_in) if k == 0 else (hidden_ref, hidden_in)
        for r in range(2):
            for i in range(rows):
                at = (r * rows + i) * cols
                x = own[0, t, 0, i] if r == 0 else far[t, i]
                xt[:, at : at + cols] = x.T
        for v in range(3):
            for r in range(2):
                lines = [above[k, t, r]] + [g_ref[k, t, r, i] for i in range(rows)] + [below[k, t, r]]
                for n, line in enumerate(lines):
                    if v != 1:
                        line = shifted(line.astype(F32), 1 - v).astype(BF16)
                    for u in range(3):
                        i = n + u - 2
                        if 0 <= i < rows:
                            at = (r * rows + i) * cols
                            yt[at : at + cols, u * channels : (u + 1) * channels] = line
            value = jnp.dot(xt[...], yt[...], preferred_element_type=F32)
            for u in range(3):
                part = value[:, u * channels : (u + 1) * channels]
                first = (u * 3 + v) * channels
                where = pl.ds(first, channels)
                if t > 0:
                    part = part + total[k, where, :]
                if t < ticks - 1:
                    total[k, where, :] = part
                    continue
                at = first
                while at < first + channels:
                    piece, offset = at // share, at % share
                    length = min(share - offset, first + channels - at)
                    term[k, piece, offset : offset + length, :] = part[
                        at - first : at - first + length
                    ].astype(BF16)
                    at += length

    def pair_start(k):
        copies = []
        for z in range(chips):
            copies.append(
                send(
                    copy(term.at[k, 2 * z + 1 - core], pair_in.at[k, z], pair_sem.at[k, z],
                         (sec, row + 1 - 2 * core))
                )
            )
        return copies

    def chip_start(k, pairs):
        for c in pairs:
            c.wait_recv()
        copies = []
        for d in range(1, chips):
            z = (chip + d) % chips
            value = term[k, 2 * z + core].astype(F32) + pair_in[k, z].astype(F32)
            pair_sum[k, d - 1] = value.astype(BF16)
            copies.append(
                send(
                    copy(pair_sum.at[k, d - 1], chip_in.at[k, d - 1], chip_sem.at[k, d - 1],
                         (sec, 2 * z + core))
                )
            )
        return copies

    def finish(k, copies):
        value = term[k, 2 * chip + core].astype(F32) + pair_in[k, chip].astype(F32)
        for d, c in enumerate(copies):
            c.wait_recv()
            value = value + chip_in[k, d].astype(F32)
        wgrads_ref[0, k] = value * scale

    is_last = sec == sections - 1
    hand = None
    backs = []
    for t in range(ticks):
        if t == 0:
            flight_copy.wait_recv()
            words_copies[0].wait_recv()
            gate(t, lambda r, i: flight_ref[0, 0, i] if r == 0 else flight_in[i])
        else:
            words_copies[t].wait_recv()
            arrive(hand, jnp.logical_not(is_last))

            @pl.when(is_last)
            def _():
                gate(t, lambda r, i: fresh_ref[r, t - 1, i])

            @pl.when(jnp.logical_not(is_last))
            def _():
                gate(t, lambda r, i: handed[t - 1, r, i])

        pairs = exchange(1, t)
        for c in queue[t] if t < len(queue) else []:
            send(c)
        arrived(pairs)
        back = transposed(g_ref.at[1, t], above.at[1, t], below.at[1, t], w_ref, 1)
        for r in range(2):
            for i in range(rows):
                g_ref[0, t, r, i] = (back[r * rows + i] * gate_of(words(r, t, 0, i))).astype(BF16)
        pairs = exchange(0, t)
        hidden_copies[t].wait_recv()
        if t == ticks - 1:
            add_terms(1, t)
            second = pair_start(1)
        arrived(pairs)
        back = transposed(g_ref.at[0, t], above.at[0, t], below.at[0, t], w_ref, 0)
        for r in range(2):
            for i in range(rows):
                value = (g_ref[1, t, r, i].astype(F32) + back[r * rows + i]).astype(BF16)
                produced[t, r, i] = value
                if r == 0:
                    grads_ref[0, t, 0, i] = value
        if t < ticks - 1:
            hand = copy(produced.at[t], handed.at[t], hand_sem.at[t], (jnp.maximum(sec - 1, 0), row))
            send(hand, sec > 0)
        backs.append(send(copy(produced.at[t, 1], grads_ref.at[1, t, 0], back_sem.at[t], other)))
        if t < ticks - 1:
            add_terms(1, t)
            if t > 0:
                inputs_copies[t - 1].wait_recv()
                add_terms(0, t - 1)
    second = chip_start(1, second)
    for t in range(ticks - 2, ticks):
        inputs_copies[t].wait_recv()
        add_terms(0, t)
    first = pair_start(0)
    first = chip_start(0, first)
    finish(1, second)
    finish(0, first)
    for c in backs:
        c.wait_recv()
    for c, when in waits:
        if when is None:
            c.wait_send()
        else:
            pl.when(when)(c.wait_send)


def per_device(in_flight, fresh, saved_inputs, saved_hidden, masks, weights):
    bands = lax.axis_size("row")
    ticks = saved_inputs.shape[1]
    rows, cols, channels = saved_inputs.shape[3:]
    chips, share = bands // 2, 9 * channels // bands
    span = 2 * rows * cols
    line = (rows, cols, channels)
    dma = pltpu.SemaphoreType.DMA
    scratch = [
        pltpu.VMEM(line, BF16),
        pltpu.VMEM((ticks,) + masks.shape[3:], jnp.int32),
        pltpu.VMEM((ticks,) + line, BF16),
        pltpu.VMEM((ticks,) + line, BF16),
        pltpu.VMEM((ticks - 1, 2) + line, BF16),
        pltpu.VMEM((ticks, 2) + line, BF16),
        pltpu.VMEM((2, ticks, 2) + line, BF16),
        pltpu.VMEM((2, ticks, 2) + line[1:], BF16),
        pltpu.VMEM((2, ticks, 2) + line[1:], BF16),
        pltpu.VMEM((2, 9 * channels, channels), F32),
        pltpu.VMEM((2, bands, share, channels), BF16),
        pltpu.VMEM((2, chips, share, channels), BF16),
        pltpu.VMEM((2, chips - 1, share, channels), BF16),
        pltpu.VMEM((2, chips - 1, share, channels), BF16),
        pltpu.VMEM((channels, span), BF16),
        pltpu.VMEM((span, 3 * channels), BF16),
        dma((2,)), dma((ticks, 2)), dma((2, ticks, 2)), dma((ticks - 1, 2)), dma((ticks, 2)),
        dma((2, ticks, 2, 2)), dma((2, ticks, 2, 2)), dma((2, chips, 2)), dma((2, chips - 1, 2)),
    ]
    return pl.pallas_call(
        relay_kernel,
        out_shape=(
            jax.ShapeDtypeStruct(saved_inputs.shape, BF16),
            jax.ShapeDtypeStruct((1, 2, share, channels), F32),
        ),
        in_specs=[VMEM] * 6,
        out_specs=(VMEM, VMEM),
        scratch_shapes=scratch,
        compiler_params=pltpu.CompilerParams(
            collective_id=0, has_side_effects=True, vmem_limit_bytes=48 << 20
        ),
    )(in_flight, fresh, saved_inputs, saved_hidden, masks, weights)


def solution(mesh):
    return jax.shard_map(
        per_device,
        mesh=mesh,
        in_specs=(
            P(None, "section", "row", None, None),
            P(None, None, "row", None, None),
            P(None, None, "section", "row", None, None),
            P(None, None, "section", "row", None, None),
            P(None, None, "section", None, "row", None, None),
            P("section", None, None, None),
        ),
        out_specs=(P(None, None, "section", "row", None, None), P("section", None, "row", None)),
        check_vma=False,
    )
```

```python
import math

import jax
import jax.numpy as jnp
from jax import lax
from jax.experimental import pallas as pl
from jax.experimental.pallas import tpu as pltpu
from jax.sharding import PartitionSpec as P

F32 = jnp.float32
BF16 = jnp.bfloat16
VMEM = pl.BlockSpec(memory_space=pltpu.VMEM)


def gate_of(words):
    groups, channels = words.shape
    bit = lax.broadcasted_iota(jnp.int32, (8, channels), 0)
    pieces = [
        jnp.bitwise_and(
            jnp.right_shift(jnp.broadcast_to(words[j : j + 1, :], (8, channels)), bit), 1
        )
        for j in range(groups)
    ]
    return jnp.concatenate(pieces, axis=0).astype(F32)


def shifted(x, step):
    cols = x.shape[0]
    rolled = pltpu.roll(x, (-step) % cols, 0)
    at = lax.broadcasted_iota(jnp.int32, x.shape, 0)
    edge = cols - 1 if step == 1 else 0
    return jnp.where(at == edge, 0.0, rolled)


def transposed(core_ref, above_ref, below_ref, w_ref):
    rows, cols, channels = core_ref.shape
    padded = [above_ref[...]] + [core_ref[i] for i in range(rows)] + [below_ref[...]]
    lhs = jnp.concatenate(
        [jnp.concatenate([padded[i - u + 2] for i in range(rows)], axis=0) for u in range(3)],
        axis=1,
    )
    parts = []
    for v in range(3):
        rhs = jnp.concatenate(
            [w_ref[pl.ds((u * 3 + v) * channels, channels), :] for u in range(3)], axis=1
        )
        parts.append(
            lax.dot_general(lhs, rhs, (((1,), (1,)), ((), ())), preferred_element_type=F32)
        )
    out = []
    for n in range(rows):
        low, mid, high = (part[n * cols : (n + 1) * cols] for part in parts)
        out.append(shifted(low, 1) + mid + shifted(high, -1))
    return out


MESH = pl.DeviceIdType.MESH


def relay_kernel(
    flight_ref, fresh_ref, inputs_ref, hidden_ref, masks_ref, w_ref,
    grads_ref, wgrads_ref,
    flight_own, fresh_own, inputs_own, hidden_own, words_own, w_own, load_sem,
    flight_in, words_in, inputs_in, hidden_in, handed, produced,
    g_ref, above, below, total, term, pair_in, pair_sum, chip_in, xt, yt,
    flight_sem, words_sem, saved_sem, hand_sem, back_sem, up_sem, down_sem, pair_sem, chip_sem,
):
    sections, bands = lax.axis_size("section"), lax.axis_size("row")
    sec, row = lax.axis_index("section"), lax.axis_index("row")
    ticks, _, rows, cols, channels = inputs_ref.shape[1:]
    chips = bands // 2
    chip, core = row // 2, row % 2
    mirror = sections - 1 - sec
    share = 9 * channels // bands
    scale = 1.0 / math.sqrt(2 * ticks * rows * bands * cols)

    loads = [
        pltpu.make_async_copy(source, target, load_sem.at[n])
        for n, (source, target) in enumerate(
            [
                (flight_ref.at[0, 0], flight_own),
                (masks_ref.at[0, :, 0], words_own),
                (w_ref.at[0, 1], w_own.at[1]),
                (w_ref.at[0, 0], w_own.at[0]),
                (fresh_ref, fresh_own),
                (hidden_ref.at[0, :, 0], hidden_own),
                (inputs_ref.at[0, :, 0], inputs_own),
            ]
        )
    ]
    for load in loads:
        load.start()
    above[...] = jnp.zeros_like(above)
    below[...] = jnp.zeros_like(below)
    barrier = pltpu.get_barrier_semaphore()
    peers = [(sec, (row + d) % bands) for d in range(1, bands)]
    peers += [(mirror, row), ((sec + 1) % sections, row), ((sec + sections - 1) % sections, row)]
    for peer in peers:
        pl.semaphore_signal(barrier, inc=1, device_id=peer, device_id_type=MESH)
    pl.semaphore_wait(barrier, len(peers))

    waits = []

    def copy(source, target, sems, device):
        return pltpu.make_async_remote_copy(
            src_ref=source, dst_ref=target, send_sem=sems.at[0], recv_sem=sems.at[1],
            device_id=device, device_id_type=MESH,
        )

    def send(c, when=None):
        if when is None:
            c.start()
        else:
            pl.when(when)(c.start)
        waits.append((c, when))
        return c

    def arrive(c, when=None):
        if when is None:
            c.wait_recv()
        else:
            pl.when(when)(c.wait_recv)

    other = (mirror, row)
    flight_copy = send(copy(flight_ref.at[1, 0], flight_in, flight_sem, other))
    words_copies = [
        copy(masks_ref.at[1, t, 0], words_in.at[t], words_sem.at[t], other) for t in range(ticks)
    ]
    hidden_copies = [
        copy(hidden_ref.at[1, t, 0], hidden_in.at[t], saved_sem.at[1, t], other)
        for t in range(ticks)
    ]
    inputs_copies = [
        copy(inputs_ref.at[1, t, 0], inputs_in.at[t], saved_sem.at[0, t], other)
        for t in range(ticks)
    ]
    send(words_copies[0])
    queue = [
        words_copies[1:2] + hidden_copies[:1] + inputs_copies[:1] + hidden_copies[1:2],
        words_copies[2:3] + inputs_copies[1:2] + hidden_copies[2:3],
        words_copies[3:] + inputs_copies[2:3] + hidden_copies[3:] + inputs_copies[3:],
    ]

    has_above, has_below = row > 0, row < bands - 1
    up_peer = (sec, jnp.maximum(row - 1, 0))
    down_peer = (sec, jnp.minimum(row + 1, bands - 1))

    def words(r, t, k, i):
        return words_own[t, k, i] if r == 0 else words_in[t, k, i]

    def exchange(k, t, r):
        up = copy(g_ref.at[k, t, r, 0], below.at[k, t, r], up_sem.at[k, t, r], up_peer)
        down = copy(g_ref.at[k, t, r, rows - 1], above.at[k, t, r], down_sem.at[k, t, r], down_peer)
        send(up, has_above)
        send(down, has_below)
        return up, down

    def arrived(pair):
        arrive(pair[0], has_below)
        arrive(pair[1], has_above)

    def gate(t, r, state):
        for i in range(rows):
            g_ref[1, t, r, i] = (state(i).astype(F32) * gate_of(words(r, t, 1, i))).astype(BF16)

    def add_terms(k, t):
        own, far = (inputs_own, inputs_in) if k == 0 else (hidden_own, hidden_in)
        for r in range(2):
            for i in range(rows):
                at = (r * rows + i) * cols
                x = (own if r == 0 else far)[t, i]
                xt[:, at : at + cols] = x.T
        for v in range(3):
            for r in range(2):
                lines = [above[k, t, r]] + [g_ref[k, t, r, i] for i in range(rows)] + [below[k, t, r]]
                for n, line in enumerate(lines):
                    if v != 1:
                        line = shifted(line.astype(F32), 1 - v).astype(BF16)
                    for u in range(3):
                        i = n + u - 2
                        if 0 <= i < rows:
                            at = (r * rows + i) * cols
                            yt[at : at + cols, u * channels : (u + 1) * channels] = line
            value = jnp.dot(xt[...], yt[...], preferred_element_type=F32)
            for u in range(3):
                part = value[:, u * channels : (u + 1) * channels]
                first = (u * 3 + v) * channels
                where = pl.ds(first, channels)
                if t > 0:
                    part = part + total[k, where, :]
                if t < ticks - 1:
                    total[k, where, :] = part
                    continue
                at = first
                while at < first + channels:
                    piece, offset = at // share, at % share
                    length = min(share - offset, first + channels - at)
                    term[k, piece, offset : offset + length, :] = part[
                        at - first : at - first + length
                    ].astype(BF16)
                    at += length

    def pair_start(k):
        copies = []
        for z in range(chips):
            copies.append(
                send(
                    copy(term.at[k, 2 * z + 1 - core], pair_in.at[k, z], pair_sem.at[k, z],
                         (sec, row + 1 - 2 * core))
                )
            )
        return copies

    def chip_start(k, pairs):
        for c in pairs:
            c.wait_recv()
        copies = []
        for d in range(1, chips):
            z = (chip + d) % chips
            value = term[k, 2 * z + core].astype(F32) + pair_in[k, z].astype(F32)
            pair_sum[k, d - 1] = value.astype(BF16)
            copies.append(
                send(
                    copy(pair_sum.at[k, d - 1], chip_in.at[k, d - 1], chip_sem.at[k, d - 1],
                         (sec, 2 * z + core))
                )
            )
        return copies

    def finish(k, copies):
        value = term[k, 2 * chip + core].astype(F32) + pair_in[k, chip].astype(F32)
        for d, c in enumerate(copies):
            c.wait_recv()
            value = value + chip_in[k, d].astype(F32)
        wgrads_ref[0, k] = value * scale

    is_last = sec == sections - 1
    hands = [None, None]
    backs = []
    loads[0].wait()
    loads[1].wait()
    for t in range(ticks):
        pairs = []
        for r in range(2):
            if t == 0:
                if r == 1:
                    flight_copy.wait_recv()
                    words_copies[0].wait_recv()
                gate(t, r, lambda i: flight_own[i] if r == 0 else flight_in[i])
            else:
                if r == 1:
                    words_copies[t].wait_recv()
                elif t == 1:
                    loads[4].wait()

                @pl.when(is_last)
                def _():
                    gate(t, r, lambda i: fresh_own[r, t - 1, i])

                @pl.when(jnp.logical_not(is_last))
                def _():
                    hands[r].wait_recv()
                    gate(t, r, lambda i: handed[t - 1, r, i])

            pairs.append(exchange(1, t, r))
            if r == 0:
                for c in queue[t] if t < len(queue) else []:
                    send(c)
            if r == 0 and t > 0:
                inputs_copies[t - 1].wait_recv()
                if t == 1:
                    loads[6].wait()
                add_terms(0, t - 1)
        for r in range(2):
            arrived(pairs[r])
            if t == 0 and r == 0:
                loads[2].wait()
            band = g_ref.at[1, t, r]
            back = transposed(band, above.at[1, t, r], below.at[1, t, r], w_own.at[1])
            for i in range(rows):
                g_ref[0, t, r, i] = (back[i] * gate_of(words(r, t, 0, i))).astype(BF16)
            pairs[r] = exchange(0, t, r)
        if t == 0:
            loads[3].wait()
        if t == ticks - 1:
            hidden_copies[t].wait_recv()
            add_terms(1, t)
            second = pair_start(1)
        for r in range(2):
            arrived(pairs[r])
            band = g_ref.at[0, t, r]
            back = transposed(band, above.at[0, t, r], below.at[0, t, r], w_own.at[0])
            for i in range(rows):
                value = (g_ref[1, t, r, i].astype(F32) + back[i]).astype(BF16)
                produced[t, r, i] = value
                if r == 0:
                    grads_ref[0, t, 0, i] = value
            if t < ticks - 1:
                hands[r] = copy(
                    produced.at[t, r], handed.at[t, r], hand_sem.at[t, r],
                    (jnp.maximum(sec - 1, 0), row),
                )
                send(hands[r], sec > 0)
        backs.append(send(copy(produced.at[t, 1], grads_ref.at[1, t, 0], back_sem.at[t], other)))
        if t < ticks - 1:
            hidden_copies[t].wait_recv()
            if t == 0:
                loads[5].wait()
            add_terms(1, t)
    second = chip_start(1, second)
    inputs_copies[ticks - 1].wait_recv()
    add_terms(0, ticks - 1)
    first = pair_start(0)
    first = chip_start(0, first)
    finish(1, second)
    finish(0, first)
    for c in backs:
        c.wait_recv()
    for c, when in waits:
        if when is None:
            c.wait_send()
        else:
            pl.when(when)(c.wait_send)


def per_device(in_flight, fresh, saved_inputs, saved_hidden, masks, weights):
    bands = lax.axis_size("row")
    ticks = saved_inputs.shape[1]
    rows, cols, channels = saved_inputs.shape[3:]
    chips, share = bands // 2, 9 * channels // bands
    span = 2 * rows * cols
    line = (rows, cols, channels)
    dma = pltpu.SemaphoreType.DMA
    scratch = [
        pltpu.VMEM(line, BF16),
        pltpu.VMEM(fresh.shape, BF16),
        pltpu.VMEM((ticks,) + line, BF16),
        pltpu.VMEM((ticks,) + line, BF16),
        pltpu.VMEM((ticks,) + masks.shape[3:], jnp.int32),
        pltpu.VMEM(weights.shape[1:], BF16),
        dma((7,)),
        pltpu.VMEM(line, BF16),
        pltpu.VMEM((ticks,) + masks.shape[3:], jnp.int32),
        pltpu.VMEM((ticks,) + line, BF16),
        pltpu.VMEM((ticks,) + line, BF16),
        pltpu.VMEM((ticks - 1, 2) + line, BF16),
        pltpu.VMEM((ticks, 2) + line, BF16),
        pltpu.VMEM((2, ticks, 2) + line, BF16),
        pltpu.VMEM((2, ticks, 2) + line[1:], BF16),
        pltpu.VMEM((2, ticks, 2) + line[1:], BF16),
        pltpu.VMEM((2, 9 * channels, channels), F32),
        pltpu.VMEM((2, bands, share, channels), BF16),
        pltpu.VMEM((2, chips, share, channels), BF16),
        pltpu.VMEM((2, chips - 1, share, channels), BF16),
        pltpu.VMEM((2, chips - 1, share, channels), BF16),
        pltpu.VMEM((channels, span), BF16),
        pltpu.VMEM((span, 3 * channels), BF16),
        dma((2,)), dma((ticks, 2)), dma((2, ticks, 2)), dma((ticks - 1, 2, 2)), dma((ticks, 2)),
        dma((2, ticks, 2, 2)), dma((2, ticks, 2, 2)), dma((2, chips, 2)), dma((2, chips - 1, 2)),
    ]
    return pl.pallas_call(
        relay_kernel,
        out_shape=(
            jax.ShapeDtypeStruct(saved_inputs.shape, BF16),
            jax.ShapeDtypeStruct((1, 2, share, channels), F32),
        ),
        in_specs=[pl.BlockSpec(memory_space=pltpu.MemorySpace.HBM)] * 6,
        out_specs=(VMEM, VMEM),
        scratch_shapes=scratch,
        compiler_params=pltpu.CompilerParams(
            collective_id=0, has_side_effects=True, vmem_limit_bytes=48 << 20
        ),
    )(in_flight, fresh, saved_inputs, saved_hidden, masks, weights)


def solution(mesh):
    return jax.shard_map(
        per_device,
        mesh=mesh,
        in_specs=(
            P(None, "section", "row", None, None),
            P(None, None, "row", None, None),
            P(None, None, "section", "row", None, None),
            P(None, None, "section", "row", None, None),
            P(None, None, "section", None, "row", None, None),
            P("section", None, None, None),
        ),
        out_specs=(P(None, None, "section", "row", None, None), P("section", None, "row", None)),
        check_vma=False,
    )
```

```python
import math

import jax
import jax.numpy as jnp
from jax import lax
from jax.experimental import pallas as pl
from jax.experimental.pallas import tpu as pltpu
from jax.sharding import PartitionSpec as P

F32 = jnp.float32
BF16 = jnp.bfloat16
VMEM = pl.BlockSpec(memory_space=pltpu.VMEM)


def gate_of(words):
    groups, channels = words.shape
    bit = lax.broadcasted_iota(jnp.int32, (8, channels), 0)
    pieces = [
        jnp.bitwise_and(
            jnp.right_shift(jnp.broadcast_to(words[j : j + 1, :], (8, channels)), bit), 1
        )
        for j in range(groups)
    ]
    return jnp.concatenate(pieces, axis=0).astype(F32)


def shifted(x, step):
    cols = x.shape[0]
    rolled = pltpu.roll(x, (-step) % cols, 0)
    at = lax.broadcasted_iota(jnp.int32, x.shape, 0)
    edge = cols - 1 if step == 1 else 0
    return jnp.where(at == edge, 0.0, rolled)


def transposed(core_ref, above_ref, below_ref, w_ref):
    rows, cols, channels = core_ref.shape
    padded = [above_ref[...]] + [core_ref[i] for i in range(rows)] + [below_ref[...]]
    lhs = jnp.concatenate(
        [jnp.concatenate([padded[i - u + 2] for i in range(rows)], axis=0) for u in range(3)],
        axis=1,
    )
    parts = []
    for v in range(3):
        rhs = jnp.concatenate(
            [w_ref[pl.ds((u * 3 + v) * channels, channels), :] for u in range(3)], axis=1
        )
        parts.append(
            lax.dot_general(lhs, rhs, (((1,), (1,)), ((), ())), preferred_element_type=F32)
        )
    out = []
    for n in range(rows):
        low, mid, high = (part[n * cols : (n + 1) * cols] for part in parts)
        out.append(shifted(low, 1) + mid + shifted(high, -1))
    return out


MESH = pl.DeviceIdType.MESH


def relay_kernel(
    flight_ref, fresh_ref, inputs_ref, hidden_ref, masks_ref, w_ref,
    grads_ref, wgrads_ref,
    flight_own, fresh_own, inputs_own, hidden_own, words_own, w_own, load_sem,
    flight_in, words_in, inputs_in, hidden_in, handed, produced,
    g_ref, above, below, total, term, pair_in, pair_sum, chip_in, xt, yt,
    flight_sem, words_sem, saved_sem, hand_sem, back_sem, up_sem, down_sem, pair_sem, chip_sem,
):
    sections, bands = lax.axis_size("section"), lax.axis_size("row")
    sec, row = lax.axis_index("section"), lax.axis_index("row")
    ticks, _, rows, cols, channels = inputs_ref.shape[1:]
    chips = bands // 2
    chip, core = row // 2, row % 2
    mirror = sections - 1 - sec
    share = 9 * channels // bands
    scale = 1.0 / math.sqrt(2 * ticks * rows * bands * cols)

    loads = [
        pltpu.make_async_copy(source, target, load_sem.at[n])
        for n, (source, target) in enumerate(
            [
                (flight_ref.at[0, 0], flight_own),
                (masks_ref.at[0, :, 0], words_own),
                (w_ref.at[0, 1], w_own.at[1]),
                (w_ref.at[0, 0], w_own.at[0]),
                (fresh_ref, fresh_own),
                (hidden_ref.at[0, :, 0], hidden_own),
                (inputs_ref.at[0, :, 0], inputs_own),
            ]
        )
    ]
    for load in loads:
        load.start()
    above[...] = jnp.zeros_like(above)
    below[...] = jnp.zeros_like(below)
    barrier = pltpu.get_barrier_semaphore()
    peers = [(sec, (row + d) % bands) for d in range(1, bands)]
    peers += [(mirror, row), ((sec + 1) % sections, row), ((sec + sections - 1) % sections, row)]
    for peer in peers:
        pl.semaphore_signal(barrier, inc=1, device_id=peer, device_id_type=MESH)
    pl.semaphore_wait(barrier, len(peers))

    waits = []

    def copy(source, target, sems, device):
        return pltpu.make_async_remote_copy(
            src_ref=source, dst_ref=target, send_sem=sems.at[0], recv_sem=sems.at[1],
            device_id=device, device_id_type=MESH,
        )

    def send(c, when=None):
        if when is None:
            c.start()
        else:
            pl.when(when)(c.start)
        waits.append((c, when))
        return c

    def arrive(c, when=None):
        if when is None:
            c.wait_recv()
        else:
            pl.when(when)(c.wait_recv)

    other = (mirror, row)
    flight_copy = send(copy(flight_ref.at[1, 0], flight_in, flight_sem, other))
    words_copies = [
        copy(masks_ref.at[1, t, 0], words_in.at[t], words_sem.at[t], other) for t in range(ticks)
    ]
    hidden_copies = [
        copy(hidden_ref.at[1, t, 0], hidden_in.at[t], saved_sem.at[1, t], other)
        for t in range(ticks)
    ]
    inputs_copies = [
        copy(inputs_ref.at[1, t, 0], inputs_in.at[t], saved_sem.at[0, t], other)
        for t in range(ticks)
    ]
    send(words_copies[0])
    queue = [
        words_copies[1:2] + hidden_copies[:1] + inputs_copies[:1] + hidden_copies[1:2],
        words_copies[2:3] + inputs_copies[1:2] + hidden_copies[2:3],
        words_copies[3:] + inputs_copies[2:3] + hidden_copies[3:] + inputs_copies[3:],
    ]

    has_above, has_below = row > 0, row < bands - 1
    up_peer = (sec, jnp.maximum(row - 1, 0))
    down_peer = (sec, jnp.minimum(row + 1, bands - 1))

    def words(r, t, k, i):
        return words_own[t, k, i] if r == 0 else words_in[t, k, i]

    def exchange(k, t, r):
        up = copy(g_ref.at[k, t, r, 0], below.at[k, t, r], up_sem.at[k, t, r], up_peer)
        down = copy(g_ref.at[k, t, r, rows - 1], above.at[k, t, r], down_sem.at[k, t, r], down_peer)
        send(up, has_above)
        send(down, has_below)
        return up, down

    def arrived(pair):
        arrive(pair[0], has_below)
        arrive(pair[1], has_above)

    def gate(t, r, state):
        for i in range(rows):
            g_ref[1, t, r, i] = (state(i).astype(F32) * gate_of(words(r, t, 1, i))).astype(BF16)

    def add_terms(k, t):
        own, far = (inputs_own, inputs_in) if k == 0 else (hidden_own, hidden_in)
        for r in range(2):
            for i in range(rows):
                at = (r * rows + i) * cols
                x = (own if r == 0 else far)[t, i]
                xt[:, at : at + cols] = x.T
        for v in range(3):
            for r in range(2):
                lines = [above[k, t, r]] + [g_ref[k, t, r, i] for i in range(rows)] + [below[k, t, r]]
                for n, line in enumerate(lines):
                    if v != 1:
                        line = shifted(line.astype(F32), 1 - v).astype(BF16)
                    for u in range(3):
                        i = n + u - 2
                        if 0 <= i < rows:
                            at = (r * rows + i) * cols
                            yt[at : at + cols, u * channels : (u + 1) * channels] = line
            value = jnp.dot(xt[...], yt[...], preferred_element_type=F32)
            for u in range(3):
                part = value[:, u * channels : (u + 1) * channels]
                first = (u * 3 + v) * channels
                where = pl.ds(first, channels)
                if t > 0:
                    part = part + total[k, where, :]
                if t < ticks - 1:
                    total[k, where, :] = part
                    continue
                at = first
                while at < first + channels:
                    piece, offset = at // share, at % share
                    length = min(share - offset, first + channels - at)
                    term[k, piece, offset : offset + length, :] = part[
                        at - first : at - first + length
                    ].astype(BF16)
                    at += length

    def pair_start(k):
        copies = []
        for z in range(chips):
            copies.append(
                send(
                    copy(term.at[k, 2 * z + 1 - core], pair_in.at[k, z], pair_sem.at[k, z],
                         (sec, row + 1 - 2 * core))
                )
            )
        return copies

    def chip_start(k, pairs):
        for c in pairs:
            c.wait_recv()
        copies = []
        for d in range(1, chips):
            z = (chip + d) % chips
            value = term[k, 2 * z + core].astype(F32) + pair_in[k, z].astype(F32)
            pair_sum[k, d - 1] = value.astype(BF16)
            copies.append(
                send(
                    copy(pair_sum.at[k, d - 1], chip_in.at[k, d - 1], chip_sem.at[k, d - 1],
                         (sec, 2 * z + core))
                )
            )
        return copies

    def finish(k, copies):
        value = term[k, 2 * chip + core].astype(F32) + pair_in[k, chip].astype(F32)
        for d, c in enumerate(copies):
            c.wait_recv()
            value = value + chip_in[k, d].astype(F32)
        wgrads_ref[0, k] = value * scale

    is_last = sec == sections - 1
    hands = [None, None]
    backs = []
    loads[0].wait()
    loads[1].wait()
    for t in range(ticks):
        pairs = []
        for r in range(2):
            if t == 0:
                if r == 1:
                    flight_copy.wait_recv()
                    words_copies[0].wait_recv()
                gate(t, r, lambda i: flight_own[i] if r == 0 else flight_in[i])
            else:
                if r == 1:
                    words_copies[t].wait_recv()
                elif t == 1:
                    loads[4].wait()

                @pl.when(is_last)
                def _():
                    gate(t, r, lambda i: fresh_own[r, t - 1, i])

                @pl.when(jnp.logical_not(is_last))
                def _():
                    hands[r].wait_recv()
                    gate(t, r, lambda i: handed[t - 1, r, i])

            pairs.append(exchange(1, t, r))
            if r == 0:
                for c in queue[t] if t < len(queue) else []:
                    send(c)
            if r == 0 and t > 0:
                inputs_copies[t - 1].wait_recv()
                if t == 1:
                    loads[6].wait()
                add_terms(0, t - 1)
        for r in range(2):
            arrived(pairs[r])
            if t == 0 and r == 0:
                loads[2].wait()
            band = g_ref.at[1, t, r]
            back = transposed(band, above.at[1, t, r], below.at[1, t, r], w_own.at[1])
            for i in range(rows):
                g_ref[0, t, r, i] = (back[i] * gate_of(words(r, t, 0, i))).astype(BF16)
            pairs[r] = exchange(0, t, r)
        if t == 0:
            loads[3].wait()
        if t == ticks - 1:
            hidden_copies[t].wait_recv()
            add_terms(1, t)
            second = pair_start(1)
        for r in range(2):
            arrived(pairs[r])
            band = g_ref.at[0, t, r]
            back = transposed(band, above.at[0, t, r], below.at[0, t, r], w_own.at[0])
            for i in range(rows):
                value = (g_ref[1, t, r, i].astype(F32) + back[i]).astype(BF16)
                produced[t, r, i] = value
                if r == 0:
                    grads_ref[0, t, 0, i] = value
            if t < ticks - 1:
                hands[r] = copy(
                    produced.at[t, r], handed.at[t, r], hand_sem.at[t, r],
                    (jnp.maximum(sec - 1, 0), row),
                )
                send(hands[r], sec > 0)
        backs.append(send(copy(produced.at[t, 1], grads_ref.at[1, t, 0], back_sem.at[t], other)))
        if t < ticks - 1:
            hidden_copies[t].wait_recv()
            if t == 0:
                loads[5].wait()
            add_terms(1, t)
    second = chip_start(1, second)
    inputs_copies[ticks - 1].wait_recv()
    add_terms(0, ticks - 1)
    first = pair_start(0)
    first = chip_start(0, first)
    finish(1, second)
    finish(0, first)
    for c in backs:
        c.wait_recv()
    for c, when in waits:
        if when is None:
            c.wait_send()
        else:
            pl.when(when)(c.wait_send)


def per_device(in_flight, fresh, saved_inputs, saved_hidden, masks, weights):
    bands = lax.axis_size("row")
    ticks = saved_inputs.shape[1]
    rows, cols, channels = saved_inputs.shape[3:]
    chips, share = bands // 2, 9 * channels // bands
    span = 2 * rows * cols
    line = (rows, cols, channels)
    dma = pltpu.SemaphoreType.DMA
    scratch = [
        pltpu.VMEM(line, BF16),
        pltpu.VMEM(fresh.shape, BF16),
        pltpu.VMEM((ticks,) + line, BF16),
        pltpu.VMEM((ticks,) + line, BF16),
        pltpu.VMEM((ticks,) + masks.shape[3:], jnp.int32),
        pltpu.VMEM(weights.shape[1:], BF16),
        dma((7,)),
        pltpu.VMEM(line, BF16),
        pltpu.VMEM((ticks,) + masks.shape[3:], jnp.int32),
        pltpu.VMEM((ticks,) + line, BF16),
        pltpu.VMEM((ticks,) + line, BF16),
        pltpu.VMEM((ticks - 1, 2) + line, BF16),
        pltpu.VMEM((ticks, 2) + line, BF16),
        pltpu.VMEM((2, ticks, 2) + line, BF16),
        pltpu.VMEM((2, ticks, 2) + line[1:], BF16),
        pltpu.VMEM((2, ticks, 2) + line[1:], BF16),
        pltpu.VMEM((2, 9 * channels, channels), F32),
        pltpu.VMEM((2, bands, share, channels), BF16),
        pltpu.VMEM((2, chips, share, channels), BF16),
        pltpu.VMEM((2, chips - 1, share, channels), BF16),
        pltpu.VMEM((2, chips - 1, share, channels), BF16),
        pltpu.VMEM((channels, span), BF16),
        pltpu.VMEM((span, 3 * channels), BF16),
        dma((2,)), dma((ticks, 2)), dma((2, ticks, 2)), dma((ticks - 1, 2, 2)), dma((ticks, 2)),
        dma((2, ticks, 2, 2)), dma((2, ticks, 2, 2)), dma((2, chips, 2)), dma((2, chips - 1, 2)),
    ]
    return pl.pallas_call(
        relay_kernel,
        out_shape=(
            jax.ShapeDtypeStruct(saved_inputs.shape, BF16),
            jax.ShapeDtypeStruct((1, 2, share, channels), F32),
        ),
        in_specs=[pl.BlockSpec(memory_space=pltpu.MemorySpace.HBM)] * 6,
        out_specs=(VMEM, VMEM),
        scratch_shapes=scratch,
        compiler_params=pltpu.CompilerParams(
            collective_id=0, has_side_effects=True, vmem_limit_bytes=67043328
        ),
    )(in_flight, fresh, saved_inputs, saved_hidden, masks, weights)


def solution(mesh):
    return jax.shard_map(
        per_device,
        mesh=mesh,
        in_specs=(
            P(None, "section", "row", None, None),
            P(None, None, "row", None, None),
            P(None, None, "section", "row", None, None),
            P(None, None, "section", "row", None, None),
            P(None, None, "section", None, "row", None, None),
            P("section", None, None, None),
        ),
        out_specs=(P(None, None, "section", "row", None, None), P("section", None, "row", None)),
        check_vma=False,
    )
```

```python
import math

import jax
import jax.numpy as jnp
from jax import lax
from jax.experimental import pallas as pl
from jax.experimental.pallas import tpu as pltpu
from jax.sharding import PartitionSpec as P

F32 = jnp.float32
BF16 = jnp.bfloat16
VMEM = pl.BlockSpec(memory_space=pltpu.VMEM)


def gate_of(words):
    groups, channels = words.shape
    bit = lax.broadcasted_iota(jnp.int32, (8, channels), 0)
    pieces = [
        jnp.bitwise_and(
            jnp.right_shift(jnp.broadcast_to(words[j : j + 1, :], (8, channels)), bit), 1
        )
        for j in range(groups)
    ]
    return jnp.concatenate(pieces, axis=0).astype(F32)


def shifted(x, step):
    cols = x.shape[0]
    rolled = pltpu.roll(x, (-step) % cols, 0)
    at = lax.broadcasted_iota(jnp.int32, x.shape, 0)
    edge = cols - 1 if step == 1 else 0
    return jnp.where(at == edge, 0.0, rolled)


def transposed(core_ref, above_ref, below_ref, w_ref):
    rows, cols, channels = core_ref.shape
    padded = [above_ref[...]] + [core_ref[i] for i in range(rows)] + [below_ref[...]]
    lhs = jnp.concatenate(
        [jnp.concatenate([padded[i - u + 2] for i in range(rows)], axis=0) for u in range(3)],
        axis=1,
    )
    parts = []
    for v in range(3):
        rhs = jnp.concatenate(
            [w_ref[pl.ds((u * 3 + v) * channels, channels), :] for u in range(3)], axis=1
        )
        parts.append(
            lax.dot_general(lhs, rhs, (((1,), (1,)), ((), ())), preferred_element_type=F32)
        )
    out = []
    for n in range(rows):
        low, mid, high = (part[n * cols : (n + 1) * cols] for part in parts)
        out.append(shifted(low, 1) + mid + shifted(high, -1))
    return out


MESH = pl.DeviceIdType.MESH


def relay_kernel(
    flight_ref, fresh_ref, inputs_ref, hidden_ref, masks_ref, w_ref,
    grads_ref, wgrads_ref,
    flight_own, fresh_own, inputs_own, hidden_own, words_own, w_own, load_sem,
    flight_in, words_in, inputs_in, hidden_in, handed, produced,
    g_ref, above, below, total, term, pair_in, pair_sum, chip_in, xt, yt,
    flight_sem, words_sem, saved_sem, hand_sem, back_sem, up_sem, down_sem, pair_sem, chip_sem,
):
    sections, bands = lax.axis_size("section"), lax.axis_size("row")
    sec, row = lax.axis_index("section"), lax.axis_index("row")
    ticks, _, rows, cols, channels = inputs_ref.shape[1:]
    chips = bands // 2
    chip, core = row // 2, row % 2
    mirror = sections - 1 - sec
    share = 9 * channels // bands
    scale = 1.0 / math.sqrt(2 * ticks * rows * bands * cols)

    loads = [
        pltpu.make_async_copy(source, target, load_sem.at[n])
        for n, (source, target) in enumerate(
            [
                (flight_ref.at[0, 0], flight_own),
                (masks_ref.at[0, :, 0], words_own),
                (w_ref.at[0, 1], w_own.at[1]),
                (w_ref.at[0, 0], w_own.at[0]),
                (fresh_ref, fresh_own),
                (hidden_ref.at[0, :, 0], hidden_own),
                (inputs_ref.at[0, :, 0], inputs_own),
            ]
        )
    ]
    for load in loads:
        load.start()
    above[...] = jnp.zeros_like(above)
    below[...] = jnp.zeros_like(below)
    barrier = pltpu.get_barrier_semaphore()
    peers = [(sec, (row + d) % bands) for d in range(1, bands)]
    peers += [(mirror, row), ((sec + 1) % sections, row), ((sec + sections - 1) % sections, row)]
    for peer in peers:
        pl.semaphore_signal(barrier, inc=1, device_id=peer, device_id_type=MESH)
    pl.semaphore_wait(barrier, len(peers))

    waits = []

    def copy(source, target, sems, device):
        return pltpu.make_async_remote_copy(
            src_ref=source, dst_ref=target, send_sem=sems.at[0], recv_sem=sems.at[1],
            device_id=device, device_id_type=MESH,
        )

    def send(c, when=None):
        if when is None:
            c.start()
        else:
            pl.when(when)(c.start)
        waits.append((c, when))
        return c

    def arrive(c, when=None):
        if when is None:
            c.wait_recv()
        else:
            pl.when(when)(c.wait_recv)

    other = (mirror, row)
    flight_copy = send(copy(flight_ref.at[1, 0], flight_in, flight_sem, other))
    words_copies = [
        copy(masks_ref.at[1, t, 0], words_in.at[t], words_sem.at[t], other) for t in range(ticks)
    ]
    hidden_copies = [
        copy(hidden_ref.at[1, t, 0], hidden_in.at[t], saved_sem.at[1, t], other)
        for t in range(ticks)
    ]
    inputs_copies = [
        copy(inputs_ref.at[1, t, 0], inputs_in.at[t], saved_sem.at[0, t], other)
        for t in range(ticks)
    ]
    send(words_copies[0])
    queue = [
        words_copies[1:2] + hidden_copies[:1] + inputs_copies[:1] + hidden_copies[1:2],
        words_copies[2:3] + inputs_copies[1:2] + hidden_copies[2:3],
        words_copies[3:] + inputs_copies[2:3] + hidden_copies[3:] + inputs_copies[3:],
    ]

    has_above, has_below = row > 0, row < bands - 1
    up_peer = (sec, jnp.maximum(row - 1, 0))
    down_peer = (sec, jnp.minimum(row + 1, bands - 1))

    def words(r, t, k, i):
        return words_own[t, k, i] if r == 0 else words_in[t, k, i]

    def exchange(k, t, r):
        up = copy(g_ref.at[k, t, r, 0], below.at[k, t, r], up_sem.at[k, t, r], up_peer)
        down = copy(g_ref.at[k, t, r, rows - 1], above.at[k, t, r], down_sem.at[k, t, r], down_peer)
        send(up, has_above)
        send(down, has_below)
        return up, down

    def arrived(pair):
        arrive(pair[0], has_below)
        arrive(pair[1], has_above)

    def gate(t, r, state):
        for i in range(rows):
            g_ref[1, t, r, i] = (state(i).astype(F32) * gate_of(words(r, t, 1, i))).astype(BF16)

    def add_terms(k, t):
        own, far = (inputs_own, inputs_in) if k == 0 else (hidden_own, hidden_in)
        for r in range(2):
            for i in range(rows):
                at = (r * rows + i) * cols
                x = (own if r == 0 else far)[t, i]
                xt[:, at : at + cols] = x.T
        for v in range(3):
            for r in range(2):
                lines = [above[k, t, r]] + [g_ref[k, t, r, i] for i in range(rows)] + [below[k, t, r]]
                for n, line in enumerate(lines):
                    if v != 1:
                        line = shifted(line.astype(F32), 1 - v).astype(BF16)
                    for u in range(3):
                        i = n + u - 2
                        if 0 <= i < rows:
                            at = (r * rows + i) * cols
                            yt[at : at + cols, u * channels : (u + 1) * channels] = line
            value = jnp.dot(xt[...], yt[...], preferred_element_type=F32)
            for u in range(3):
                part = value[:, u * channels : (u + 1) * channels]
                first = (u * 3 + v) * channels
                where = pl.ds(first, channels)
                if t > 0:
                    part = part + total[k, where, :]
                if t < ticks - 1:
                    total[k, where, :] = part
                    continue
                at = first
                while at < first + channels:
                    piece, offset = at // share, at % share
                    length = min(share - offset, first + channels - at)
                    term[k, piece, offset : offset + length, :] = part[
                        at - first : at - first + length
                    ].astype(BF16)
                    at += length

    def pair_start(k):
        copies = []
        for z in range(chips):
            copies.append(
                send(
                    copy(term.at[k, 2 * z + 1 - core], pair_in.at[k, z], pair_sem.at[k, z],
                         (sec, row + 1 - 2 * core))
                )
            )
        return copies

    def chip_start(k, pairs):
        for c in pairs:
            c.wait_recv()
        copies = []
        for d in range(1, chips):
            z = (chip + d) % chips
            value = term[k, 2 * z + core].astype(F32) + pair_in[k, z].astype(F32)
            pair_sum[k, d - 1] = value.astype(BF16)
            copies.append(
                send(
                    copy(pair_sum.at[k, d - 1], chip_in.at[k, d - 1], chip_sem.at[k, d - 1],
                         (sec, 2 * z + core))
                )
            )
        return copies

    def finish(k, copies):
        value = term[k, 2 * chip + core].astype(F32) + pair_in[k, chip].astype(F32)
        for d, c in enumerate(copies):
            c.wait_recv()
            value = value + chip_in[k, d].astype(F32)
        wgrads_ref[0, k] = value * scale

    def back_copy(t):
        return copy(produced.at[t, 1], grads_ref.at[1, t, 0], back_sem.at[t], other)

    is_last = sec == sections - 1
    hands = [None, None]
    backs = []
    loads[0].wait()
    loads[1].wait()
    for t in range(ticks):
        pairs = []
        for r in range(2):
            if t == 0:
                if r == 1:
                    flight_copy.wait_recv()
                    words_copies[0].wait_recv()
                gate(t, r, lambda i: flight_own[i] if r == 0 else flight_in[i])
            else:
                if r == 1:
                    words_copies[t].wait_recv()
                elif t == 1:
                    loads[4].wait()

                @pl.when(is_last)
                def _():
                    gate(t, r, lambda i: fresh_own[r, t - 1, i])

                @pl.when(jnp.logical_not(is_last))
                def _():
                    hands[r].wait_recv()
                    gate(t, r, lambda i: handed[t - 1, r, i])

            pairs.append(exchange(1, t, r))
            if r == 1 and t > 0:
                backs.append(send(back_copy(t - 1)))
            if r == 0:
                for c in queue[t] if t < len(queue) else []:
                    send(c)
            if r == 0 and t > 0:
                inputs_copies[t - 1].wait_recv()
                if t == 1:
                    loads[6].wait()
                add_terms(0, t - 1)
        for r in range(2):
            arrived(pairs[r])
            if t == 0 and r == 0:
                loads[2].wait()
            band = g_ref.at[1, t, r]
            back = transposed(band, above.at[1, t, r], below.at[1, t, r], w_own.at[1])
            for i in range(rows):
                g_ref[0, t, r, i] = (back[i] * gate_of(words(r, t, 0, i))).astype(BF16)
            pairs[r] = exchange(0, t, r)
        if t == 0:
            loads[3].wait()
        if t == ticks - 1:
            hidden_copies[t].wait_recv()
            add_terms(1, t)
            second = pair_start(1)
        for r in range(2):
            arrived(pairs[r])
            band = g_ref.at[0, t, r]
            back = transposed(band, above.at[0, t, r], below.at[0, t, r], w_own.at[0])
            for i in range(rows):
                value = (g_ref[1, t, r, i].astype(F32) + back[i]).astype(BF16)
                produced[t, r, i] = value
                if r == 0:
                    grads_ref[0, t, 0, i] = value
            if t < ticks - 1:
                hands[r] = copy(
                    produced.at[t, r], handed.at[t, r], hand_sem.at[t, r],
                    (jnp.maximum(sec - 1, 0), row),
                )
                send(hands[r], sec > 0)
        if t == ticks - 1:
            backs.append(send(back_copy(t)))
        if t < ticks - 1:
            hidden_copies[t].wait_recv()
            if t == 0:
                loads[5].wait()
            add_terms(1, t)
    second = chip_start(1, second)
    inputs_copies[ticks - 1].wait_recv()
    add_terms(0, ticks - 1)
    first = pair_start(0)
    first = chip_start(0, first)
    finish(1, second)
    finish(0, first)
    for c in backs:
        c.wait_recv()
    for c, when in waits:
        if when is None:
            c.wait_send()
        else:
            pl.when(when)(c.wait_send)


def per_device(in_flight, fresh, saved_inputs, saved_hidden, masks, weights):
    bands = lax.axis_size("row")
    ticks = saved_inputs.shape[1]
    rows, cols, channels = saved_inputs.shape[3:]
    chips, share = bands // 2, 9 * channels // bands
    span = 2 * rows * cols
    line = (rows, cols, channels)
    dma = pltpu.SemaphoreType.DMA
    scratch = [
        pltpu.VMEM(line, BF16),
        pltpu.VMEM(fresh.shape, BF16),
        pltpu.VMEM((ticks,) + line, BF16),
        pltpu.VMEM((ticks,) + line, BF16),
        pltpu.VMEM((ticks,) + masks.shape[3:], jnp.int32),
        pltpu.VMEM(weights.shape[1:], BF16),
        dma((7,)),
        pltpu.VMEM(line, BF16),
        pltpu.VMEM((ticks,) + masks.shape[3:], jnp.int32),
        pltpu.VMEM((ticks,) + line, BF16),
        pltpu.VMEM((ticks,) + line, BF16),
        pltpu.VMEM((ticks - 1, 2) + line, BF16),
        pltpu.VMEM((ticks, 2) + line, BF16),
        pltpu.VMEM((2, ticks, 2) + line, BF16),
        pltpu.VMEM((2, ticks, 2) + line[1:], BF16),
        pltpu.VMEM((2, ticks, 2) + line[1:], BF16),
        pltpu.VMEM((2, 9 * channels, channels), F32),
        pltpu.VMEM((2, bands, share, channels), BF16),
        pltpu.VMEM((2, chips, share, channels), BF16),
        pltpu.VMEM((2, chips - 1, share, channels), BF16),
        pltpu.VMEM((2, chips - 1, share, channels), BF16),
        pltpu.VMEM((channels, span), BF16),
        pltpu.VMEM((span, 3 * channels), BF16),
        dma((2,)), dma((ticks, 2)), dma((2, ticks, 2)), dma((ticks - 1, 2, 2)), dma((ticks, 2)),
        dma((2, ticks, 2, 2)), dma((2, ticks, 2, 2)), dma((2, chips, 2)), dma((2, chips - 1, 2)),
    ]
    return pl.pallas_call(
        relay_kernel,
        out_shape=(
            jax.ShapeDtypeStruct(saved_inputs.shape, BF16),
            jax.ShapeDtypeStruct((1, 2, share, channels), F32),
        ),
        in_specs=[pl.BlockSpec(memory_space=pltpu.MemorySpace.HBM)] * 6,
        out_specs=(VMEM, VMEM),
        scratch_shapes=scratch,
        compiler_params=pltpu.CompilerParams(
            collective_id=0, has_side_effects=True, vmem_limit_bytes=67043328
        ),
    )(in_flight, fresh, saved_inputs, saved_hidden, masks, weights)


def solution(mesh):
    return jax.shard_map(
        per_device,
        mesh=mesh,
        in_specs=(
            P(None, "section", "row", None, None),
            P(None, None, "row", None, None),
            P(None, None, "section", "row", None, None),
            P(None, None, "section", "row", None, None),
            P(None, None, "section", None, "row", None, None),
            P("section", None, None, None),
        ),
        out_specs=(P(None, None, "section", "row", None, None), P("section", None, "row", None)),
        check_vma=False,
    )
```
